32 devices in a mesh: outer: 8 (over z, core), inner: 4 (over y, x).
Axes of the slice: x: 2, y: 2, z: 4, core: 2. Of those that a mesh axis runs over, the one named last changes fastest.
Arguments:
- leaf_blocks: float32 [32, 512, 512], P(('outer', 'inner')), as said below
- leaf_bases: float32 [32, 512, 256], P(('outer', 'inner'))
- local_gens: float32 [32, 2, 256, 256], P(('outer', 'inner'))
- chain_gens: float32 [64, 2, 256, 256], P(('outer', 'inner')), as said below
- node_ranks: int32 [3, 32], replicated, may hold values from 192 to 256, as said below
Outputs:
- local_reduced: float32 [32, 256, 256], P(('outer', 'inner'))
- chain_reduced: float32 [64, 256, 256], P(('outer', 'inner'))
- top_factor: float32 [16384, 512], P(('outer', 'inner'))
The draws below stay inside these ranges and needn't reach their ends.
Inputs may be any that keep to these rules, and one draw needn't show every extreme that they name: `node_ranks`: ranks of all tree levels, entry [v, k] read for k < 32 >> v; both ends of the range occur in every draw. `leaf_blocks`: each leaf block is symmetric positive definite. Rows of chain_gens that belong to the same node are equal on all devices below that node.
All inputs are finite; a program needn't handle non-finite values.
Results may differ from the reference program's by a relative error of at most 0.00017.
Values sent between devices are 32-bit elements; how exact they have to be, the bound alone decides.
A program may use at most 128 MiB of HBM per device.

```python
import math
import jax
import jax.numpy as jnp
from jax import lax

RANK = 256
LEAF = 512
LEAF_DEV = 1
LOCAL_LEVELS = 0
IN_LEVELS = 2
LEVELS = 3
LOCAL_NODES = 1
LEAVES = 32
DEVICES = 32


def random_noise(key, shape):
    return jax.random.normal(key, shape, jnp.float32)


def node_gens(key, level_id, node_id):
    node_key = jax.random.fold_in(jax.random.fold_in(key, level_id + 101), node_id)
    key_transfer, key_diagonal, key_coupling = jax.random.split(node_key, 3)
    row_ids = jnp.arange(RANK, dtype=jnp.int32)[:, None]
    col_ids = jnp.arange(RANK, dtype=jnp.int32)[None, :]
    is_odd = node_id % 2 == 1
    target = jnp.where(is_odd, 2 * col_ids - RANK, 2 * col_ids)
    in_half = jnp.where(is_odd, col_ids >= RANK // 2, col_ids < RANK // 2)
    dominant = ((row_ids == target) & in_half).astype(jnp.float32)
    transfer = dominant + random_noise(key_transfer, (RANK, RANK)) * (0.25 / math.sqrt(2 * RANK))
    diagonal = jax.random.uniform(key_diagonal, (RANK,), jnp.float32, -0.25, 0.25)
    coupling = jnp.diag(diagonal) + random_noise(key_coupling, (RANK, RANK)) * (0.06 / math.sqrt(RANK))
    return jnp.stack([transfer, coupling])


def draw_leaf_blocks(key, part):
    key_diagonal, key_noise = jax.random.split(jax.random.fold_in(key, 11))
    diagonal = jnp.exp(jax.random.uniform(key_diagonal, (LEAVES, LEAF), jnp.float32, math.log(3.0), math.log(8.0)))
    random_part = random_noise(key_noise, (LEAVES, LEAF, LEAF))
    symmetric = (random_part + jnp.swapaxes(random_part, 1, 2)) * (1.0 / math.sqrt(2.0 * LEAF))
    return symmetric + diagonal[:, :, None] * jnp.eye(LEAF, dtype=jnp.float32)[None, :, :]


def draw_leaf_bases(key, part):
    key_noise = jax.random.fold_in(key, 12)
    row_ids = jnp.arange(LEAF, dtype=jnp.int32)[:, None]
    col_ids = jnp.arange(RANK, dtype=jnp.int32)[None, :]
    dominant = (row_ids == 2 * col_ids).astype(jnp.float32)
    return dominant[None, :, :] + random_noise(key_noise, (LEAVES, LEAF, RANK)) * (0.25 / math.sqrt(LEAF))


def draw_local_gens(key, part):
    levels, positions, counts = ([], [], [])
    for tree_level in range(LOCAL_LEVELS + 1):
        per_device = LEAF_DEV >> tree_level
        for position in range(per_device):
            levels.append(tree_level)
            positions.append(position)
            counts.append(per_device)
    device = jnp.arange(DEVICES, dtype=jnp.int32)[:, None]
    level_ids = jnp.broadcast_to(jnp.array(levels, jnp.int32)[None, :], (DEVICES, LOCAL_NODES))
    node_ids = device * jnp.array(counts, jnp.int32)[None, :] + jnp.array(positions, jnp.int32)[None, :]
    gen_key = jax.random.fold_in(key, 13)
    return jax.vmap(lambda level_id, node_id: node_gens(gen_key, level_id, node_id))(level_ids.reshape(-1), node_ids.reshape(-1))


def draw_chain_gens(key, part):
    device = jnp.arange(DEVICES, dtype=jnp.int32)[:, None]
    depths = jnp.arange(1, IN_LEVELS + 1, dtype=jnp.int32)[None, :]
    level_ids = jnp.broadcast_to(LOCAL_LEVELS + depths, (DEVICES, IN_LEVELS))
    node_ids = jnp.right_shift(device, depths)
    gen_key = jax.random.fold_in(key, 13)
    return jax.vmap(lambda level_id, node_id: node_gens(gen_key, level_id, node_id))(level_ids.reshape(-1), node_ids.reshape(-1))


def draw_node_ranks(key, part):
    ranks = jax.random.randint(jax.random.fold_in(key, 14), (LEVELS, LEAVES), 3 * RANK // 4, RANK + 1, jnp.int32)
    return ranks.at[0, 0].set(RANK).at[0, 1].set(3 * RANK // 4)


def setup_inputs(seed: int = 0) -> dict:
    keys = jax.random.split(jax.random.key(seed), 6)
    return {
        "leaf_blocks": draw_leaf_blocks(jax.random.fold_in(keys[5], 71), 0),
        "leaf_bases": draw_leaf_bases(jax.random.fold_in(keys[5], 71), 0),
        "local_gens": draw_local_gens(jax.random.fold_in(keys[5], 71), 0),
        "chain_gens": draw_chain_gens(jax.random.fold_in(keys[5], 71), 0),
        "node_ranks": draw_node_ranks(jax.random.fold_in(keys[5], 71), 0),
    }


PRECISE = lax.Precision.HIGHEST

def column_mask(ranks, rank_width):
    return (jnp.arange(rank_width, dtype=jnp.int32)[None, :] < ranks[:, None]).astype(jnp.float32)

def reduce_node(node_block, node_basis, col_mask):
    factor = jnp.linalg.cholesky(node_block)
    whitened = lax.linalg.triangular_solve(factor, node_basis, left_side=True, lower=True)
    gram_matrix = jnp.dot(whitened.T, whitened, precision=PRECISE) + jnp.diag(1.0 - col_mask)
    gram_factor = jnp.linalg.cholesky(gram_matrix)
    identity = jnp.eye(col_mask.shape[0], dtype=jnp.float32)
    inverse_factor = lax.linalg.triangular_solve(gram_factor, identity, left_side=True, lower=True)
    reduced = jnp.dot(inverse_factor.T, inverse_factor, precision=PRECISE)
    return reduced * col_mask[:, None] * col_mask[None, :]

def assemble(reduced_left, reduced_right, couple_left, couple_right, mask_left, mask_right):
    coupling = (couple_left + couple_right.T) * mask_left[:, None] * mask_right[None, :]
    upper_half = jnp.concatenate([reduced_left, coupling], axis=1)
    lower_half = jnp.concatenate([coupling.T, reduced_right], axis=1)
    row_mask = jnp.concatenate([mask_left, mask_right])
    node_block = jnp.concatenate([upper_half, lower_half], axis=0) + jnp.diag(1.0 - row_mask)
    return (node_block, row_mask)

def merge_pair(reduced_left, reduced_right, gens_left, gens_right, mask_left, mask_right, mask_parent):
    node_block, row_mask = assemble(reduced_left, reduced_right, gens_left[1], gens_right[1], mask_left, mask_right)
    node_basis = jnp.concatenate([gens_left[0], gens_right[0]], axis=0) * row_mask[:, None] * mask_parent[None, :]
    return reduce_node(node_block, node_basis, mask_parent)

def reference(leaf_blocks, leaf_bases, local_gens, chain_gens, node_ranks):
    rank_width = RANK
    local_all = local_gens.reshape(DEVICES, 2 * LEAF_DEV - 1, 2, rank_width, rank_width)
    chain_all = chain_gens.reshape(DEVICES, IN_LEVELS, 2, rank_width, rank_width)
    col_mask = column_mask(node_ranks[0], rank_width)
    reduced = lax.map(lambda element: reduce_node(element[0], element[1] * element[2][None, :], element[2]), (leaf_blocks, leaf_bases, col_mask))
    local_parts = [reduced.reshape(DEVICES, LEAF_DEV, rank_width, rank_width)]
    chain_parts = []
    offset = 0
    top_blocks = None
    for tree_level in range(LOCAL_LEVELS + IN_LEVELS + 1):
        node_count = LEAVES >> tree_level
        if tree_level <= LOCAL_LEVELS:
            per_device = LEAF_DEV >> tree_level
            generators = local_all[:, offset:offset + per_device].reshape(node_count, 2, rank_width, rank_width)
            offset = offset + per_device
        else:
            group_depth = tree_level - LOCAL_LEVELS
            generators = chain_all[::2 ** group_depth, group_depth - 1]
        col_mask = column_mask(node_ranks[tree_level, :node_count], rank_width)
        pair_args = (reduced[0::2], reduced[1::2], generators[0::2], generators[1::2], col_mask[0::2], col_mask[1::2])
        if tree_level == LOCAL_LEVELS + IN_LEVELS:
            top_blocks = lax.map(lambda element: jnp.linalg.cholesky(assemble(element[0], element[1], element[2][1], element[3][1], element[4], element[5])[0]), pair_args)
        else:
            parent_mask = column_mask(node_ranks[tree_level + 1, :node_count // 2], rank_width)
            reduced = lax.map(lambda element: merge_pair(*element), pair_args + (parent_mask,))
            if tree_level + 1 <= LOCAL_LEVELS:
                local_parts.append(reduced.reshape(DEVICES, LEAF_DEV >> tree_level + 1, rank_width, rank_width))
            else:
                chain_parts.append(jnp.repeat(reduced, 2 ** (tree_level + 1 - LOCAL_LEVELS), axis=0))
    local_reduced = jnp.concatenate(local_parts, axis=1).reshape(DEVICES * (2 * LEAF_DEV - 1), rank_width, rank_width)
    chain_reduced = jnp.stack(chain_parts, axis=1).reshape(DEVICES * IN_LEVELS, rank_width, rank_width)
    top_factor = jnp.repeat(top_blocks, 2 ** (IN_LEVELS + 1), axis=0).reshape(DEVICES * 2 * rank_width, 2 * rank_width)
    return (local_reduced, chain_reduced, top_factor)
```

```python
import functools

import jax
import jax.numpy as jnp
from jax import lax
from jax.experimental import pallas as pl
from jax.experimental.pallas import tpu as pltpu
from jax.sharding import PartitionSpec as P

LANES = 128
SUB = 8
PANEL = 32
HIGH = lax.Precision.HIGHEST


def dot(a, b, dims=((1,), (0,))):
    return lax.dot_general(a, b, (dims, ((), ())), precision=HIGH, preferred_element_type=jnp.float32)


NT = ((1,), (1,))
TN = ((0,), (0,))


def iota(shape, axis):
    return lax.broadcasted_iota(jnp.int32, shape, axis)


def row_of(x, j):
    return jnp.broadcast_to(x[j : j + 1, :], x.shape)


def col_of(x, c):
    return jnp.broadcast_to(x[:, c : c + 1], x.shape)


def eliminate(a_ref, pad_ref, keep_ref=None, reverse=False):
    n = a_ref.shape[0]
    tiles = n // LANES
    groups = PANEL // SUB
    sub = iota((SUB, LANES), 0)
    lane = iota((SUB, LANES), 1)
    wide = iota((n, LANES), 1)
    pad_ref[...] = jnp.zeros_like(pad_ref)

    def order(count):
        return range(count - 1, -1, -1) if reverse else range(count)

    def tile_step(step, carry):
        h = tiles - 1 - step if reverse else step
        own_at = pl.multiple_of(h * LANES, LANES)
        spots = [own_at] + [pl.multiple_of(lax.rem(h + t, tiles) * LANES, LANES) for t in range(1, tiles)]
        for q in order(LANES // PANEL):
            base_row = pl.multiple_of(h * LANES + q * PANEL, PANEL)
            rows = [
                [a_ref[pl.ds(pl.multiple_of(base_row + g * SUB, SUB), SUB), pl.ds(spot, LANES)] for spot in spots]
                for g in range(groups)
            ]
            for s in order(groups):
                c0 = q * PANEL + s * SUB
                cols = [col_of(rows[s][0], c0 + j) for j in range(SUB)]
                other = {g: [col_of(rows[g][0], c0 + j) for j in range(SUB)] for g in range(groups) if g != s}
                piv = list(rows[s])
                kept = [jnp.zeros((SUB, LANES), jnp.float32) for _ in spots]
                seen = []
                for j in order(SUB):
                    seen.append(j)
                    p = row_of(cols[j], j)
                    inv = 1.0 / p
                    here = lane == c0 + j
                    at = sub == j
                    lines = [row_of(x, j) for x in piv]
                    if keep_ref is not None:
                        root = lax.rsqrt(p)
                        kept = [jnp.where(at, x * root, k) for x, k in zip(lines, kept)]
                    lines[0] = jnp.where(here, 1.0, lines[0])
                    piv[0] = jnp.where(here, 0.0, piv[0])
                    lines = [x * inv for x in lines]
                    piv = [jnp.where(at, x, y - cols[j] * x) for x, y in zip(lines, piv)]
                    for i in range(SUB):
                        if i not in seen:
                            line = row_of(cols[i], j) * inv
                            cols[i] = jnp.where(at, line, cols[i] - cols[j] * line)
                rows[s] = piv
                if keep_ref is not None:
                    for spot, k in zip(spots, kept):
                        keep_ref[pl.ds(pl.multiple_of(base_row + s * SUB, SUB), SUB), pl.ds(spot, LANES)] = k
                spread = [[row_of(x, j) for j in range(SUB)] for x in piv]
                inside = (lane >= c0) & (lane < c0 + SUB)
                for g, mult in other.items():
                    new = list(rows[g])
                    new[0] = jnp.where(inside, 0.0, new[0])
                    for j in range(SUB):
                        new = [x - mult[j] * y[j] for x, y in zip(new, spread)]
                    rows[g] = new
            for g in range(groups):
                for spot, x in zip(spots, rows[g]):
                    pad_ref[q * PANEL + g * SUB : q * PANEL + (g + 1) * SUB, pl.ds(spot, LANES)] = x
            in_panel = (wide >= q * PANEL) & (wide < (q + 1) * PANEL)
            own = a_ref[:, pl.ds(own_at, LANES)]
            lhs = jnp.where(in_panel, own, 0.0)
            a_ref[:, pl.ds(own_at, LANES)] = jnp.where(in_panel, 0.0, own)
            a_ref[...] = a_ref[...] - dot(lhs, pad_ref[...])
            for g in range(groups):
                for spot, x in zip(spots, rows[g]):
                    a_ref[pl.ds(pl.multiple_of(base_row + g * SUB, SUB), SUB), pl.ds(spot, LANES)] = x
        return carry

    lax.fori_loop(0, tiles, tile_step, 0)


def unit_rest(n, rank):
    return jnp.where((iota((n, n), 0) == iota((n, n), 1)) & (iota((n, n), 0) >= rank), 1.0, 0.0)


def both(n, rank_row, rank_col, x):
    return jnp.where((iota((n, n), 0) < rank_row) & (iota((n, n), 1) < rank_col), x, 0.0)


def leaf_kernel(rank_ref, m_ref, v_ref, g_ref, a_ref, pad_ref):
    n = g_ref.shape[0]
    rank = rank_ref[0]
    keep = iota((n, n), 1) < rank
    v1 = jnp.where(keep, v_ref[:n, :], 0.0)
    v2 = jnp.where(keep, v_ref[n:, :], 0.0)
    a_ref[...] = m_ref[n:, n:]
    eliminate(a_ref, pad_ref)
    m12 = m_ref[:n, n:]
    w = dot(m12, a_ref[...])
    t = dot(a_ref[...], v2)
    a_ref[...] = m_ref[:n, :n] - dot(w, m12, NT)
    y = v1 - dot(w, v2)
    eliminate(a_ref, pad_ref)
    g_ref[...] = dot(v2, t, TN) + dot(y, dot(a_ref[...], y), TN) + unit_rest(n, rank)


def invert_kernel(rank_ref, g_ref, l_ref, a_ref, pad_ref):
    n = g_ref.shape[0]
    rank = rank_ref[0]
    a_ref[...] = g_ref[...]
    eliminate(a_ref, pad_ref)
    l_ref[...] = both(n, rank, rank, a_ref[...])


def merge_kernel(rank_ref, l_ref, gy_ref, mine_ref, theirs_ref, g_ref, a_ref, pad_ref):
    n = g_ref.shape[0]
    rx, ry, rp = rank_ref[0], rank_ref[1], rank_ref[2]
    couple = both(n, rx, ry, mine_ref[1] + theirs_ref[1].T)
    px = both(n, rx, rp, mine_ref[0])
    py = both(n, ry, rp, theirs_ref[0])
    gy = gy_ref[...]
    w = dot(couple, gy)
    a_ref[...] = l_ref[...] + unit_rest(n, rx) - dot(w, couple, NT)
    y = px - dot(w, py)
    t = dot(py, dot(gy, py), TN)
    eliminate(a_ref, pad_ref)
    g_ref[...] = t + dot(y, dot(a_ref[...], y), TN) + unit_rest(n, rp)


def top_kernel(rank_ref, la_ref, lb_ref, ca_ref, cb_ref, f_ref, a_ref, pad_ref, e_ref):
    n = la_ref.shape[0]
    ra, rb = rank_ref[0], rank_ref[1]
    row, col = iota((n, n), 0), iota((n, n), 1)
    couple = both(n, ra, rb, ca_ref[...] + cb_ref[...].T)
    a_ref[...] = la_ref[...] + unit_rest(n, ra)
    eliminate(a_ref, pad_ref, e_ref)
    e = e_ref[...]
    f_ref[:n, :n] = jnp.where(row <= col, e, 0.0).T
    f_ref[:n, n:] = jnp.zeros((n, n), jnp.float32)
    diag = jnp.where(row == col, e, 0.0)
    lower = jnp.where(row > col, e, 0.0) + jnp.where(row == col, 1.0 / jnp.where(row == col, e, 1.0), 0.0)
    f21 = dot(couple, lower, ((0,), (1,)))
    f_ref[n:, :n] = f21
    a_ref[...] = lb_ref[...] + unit_rest(n, rb) - dot(f21, f21, NT)
    eliminate(a_ref, pad_ref, e_ref)
    f_ref[n:, n:] = jnp.where(row <= col, e_ref[...], 0.0).T


def call(kernel, name, out_shape, n, ranks, *arrays, keep=False):
    vmem = pl.BlockSpec(memory_space=pltpu.VMEM)
    scratch = [pltpu.VMEM((n, n), jnp.float32), pltpu.VMEM((LANES, n), jnp.float32)]
    if keep:
        scratch.append(pltpu.VMEM((n, n), jnp.float32))
    return pl.pallas_call(
        kernel,
        name=name,
        out_shape=jax.ShapeDtypeStruct(out_shape, jnp.float32),
        in_specs=[pl.BlockSpec(memory_space=pltpu.SMEM)] + [vmem] * len(arrays),
        out_specs=vmem,
        scratch_shapes=scratch,
        cost_estimate=pl.CostEstimate(flops=4 * 10**9, bytes_accessed=4 * 10**6, transcendentals=0),
    )(ranks, *arrays)


def partner(x, axis, bit):
    return lax.ppermute(x, axis, [(i, i ^ 1 << bit) for i in range(lax.axis_size(axis))])


def body(leaf_blocks, leaf_bases, local_gens, chain_gens, node_ranks):
    n = leaf_bases.shape[2]
    in_levels = chain_gens.shape[0]
    inner_size = lax.axis_size("inner")
    outer_pos = lax.axis_index("outer")
    device = outer_pos * inner_size + lax.axis_index("inner")

    def rank_at(level, node):
        return lax.dynamic_slice(node_ranks, (level, node), (1, 1))[0]

    gens = [local_gens[0]] + [chain_gens[d] for d in range(in_levels)]
    others = [partner(gens[d], "inner", d) for d in range(in_levels)]
    other_couple = partner(gens[in_levels][1], "outer", 0)
    rank = rank_at(0, device)
    g = call(leaf_kernel, "leaf", (n, n), n, rank, leaf_blocks[0], leaf_bases[0])
    reduced = []
    for depth in range(in_levels):
        node = jnp.right_shift(device, depth)
        g_other = partner(g, "inner", depth)
        mine = call(invert_kernel, "invert", (n, n), n, rank, g)
        reduced.append(mine)
        up = rank_at(depth + 1, jnp.right_shift(node, 1))
        ranks = jnp.concatenate([rank, rank_at(depth, node ^ 1), up])
        g = call(merge_kernel, "merge", (n, n), n, ranks, mine, g_other, gens[depth], others[depth])
        rank = up
    mine = call(invert_kernel, "invert", (n, n), n, rank, g)
    reduced.append(mine)
    theirs = partner(mine, "outer", 0)
    other_rank = rank_at(in_levels, outer_pos ^ 1)
    is_left = jnp.bitwise_and(outer_pos, 1) == 0

    def ordered(x, y):
        return jnp.where(is_left, x, y), jnp.where(is_left, y, x)

    la, lb = ordered(mine, theirs)
    ca, cb = ordered(gens[in_levels][1], other_couple)
    ranks = jnp.concatenate(ordered(rank, other_rank))
    top = call(top_kernel, "top", (2 * n, 2 * n), n, ranks, la, lb, ca, cb, keep=True)
    return (reduced[0][None], jnp.stack(reduced[1:], axis=0), top)


def solution(mesh):
    return jax.shard_map(
        body,
        mesh=mesh,
        in_specs=(
            P(("outer", "inner"), None, None),
            P(("outer", "inner"), None, None),
            P(("outer", "inner"), None, None, None),
            P(("outer", "inner"), None, None, None),
            P(),
        ),
        out_specs=(
            P(("outer", "inner"), None, None),
            P(("outer", "inner"), None, None),
            P(("outer", "inner"), None),
        ),
        check_vma=False,
    )
```

```python
import functools

import jax
import jax.numpy as jnp
from jax import lax
from jax.experimental import pallas as pl
from jax.experimental.pallas import tpu as pltpu
from jax.sharding import PartitionSpec as P

LANES = 128
SUB = 8
PANEL = 32
HIGH = lax.Precision.HIGHEST


def dot(a, b, dims=((1,), (0,))):
    return lax.dot_general(a, b, (dims, ((), ())), precision=HIGH, preferred_element_type=jnp.float32)


NT = ((1,), (1,))
TN = ((0,), (0,))


def thirds(x):
    a = x.astype(jnp.bfloat16)
    x = x - a.astype(jnp.float32)
    b = x.astype(jnp.bfloat16)
    return a, b, (x - b.astype(jnp.float32)).astype(jnp.bfloat16)


def bdot(a, b):
    return jnp.dot(a, b, preferred_element_type=jnp.float32)


def iota(shape, axis):
    return lax.broadcasted_iota(jnp.int32, shape, axis)


def row_of(x, j):
    return jnp.broadcast_to(x[j : j + 1, :], x.shape)


def col_of(x, c):
    return jnp.broadcast_to(x[:, c : c + 1], x.shape)


def eliminate(a_ref, keep_ref=None, reverse=False):
    n = a_ref.shape[0]
    tiles = n // LANES
    groups = PANEL // SUB
    sub = iota((SUB, LANES), 0)
    lane = iota((SUB, LANES), 1)
    wide = iota((n, LANES), 1)

    def order(count):
        return range(count - 1, -1, -1) if reverse else range(count)

    def tile_step(step, carry):
        h = tiles - 1 - step if reverse else step
        own_at = pl.multiple_of(h * LANES, LANES)
        spots = [own_at] + [pl.multiple_of(lax.rem(h + t, tiles) * LANES, LANES) for t in range(1, tiles)]
        for q in order(LANES // PANEL):
            base_row = pl.multiple_of(h * LANES + q * PANEL, PANEL)
            rows = [
                [a_ref[pl.ds(pl.multiple_of(base_row + g * SUB, SUB), SUB), pl.ds(spot, LANES)] for spot in spots]
                for g in range(groups)
            ]
            for s in order(groups):
                c0 = q * PANEL + s * SUB
                cols = [col_of(rows[s][0], c0 + j) for j in range(SUB)]
                other = {g: [col_of(rows[g][0], c0 + j) for j in range(SUB)] for g in range(groups) if g != s}
                piv = list(rows[s])
                kept = [jnp.zeros((SUB, LANES), jnp.float32) for _ in spots]
                left = list(order(SUB))
                inv = 1.0 / row_of(cols[left[0]], left[0])
                while left:
                    j = left.pop(0)
                    here = lane == c0 + j
                    at = sub == j
                    lines = [row_of(x, j) for x in piv]
                    if keep_ref is not None:
                        root = lax.rsqrt(row_of(cols[j], j))
                        kept = [jnp.where(at, x * root, k) for x, k in zip(lines, kept)]
                    mult = jnp.where(at, -1.0, cols[j])
                    now = inv
                    if left:
                        i = left[0]
                        cross = row_of(cols[i], j)
                        inv = 1.0 / (row_of(cols[i], i) - (cross * now) * row_of(cols[j], i))
                    lines = [jnp.where(here, 1.0, lines[0])] + lines[1:]
                    bases = [jnp.where(at | here, 0.0, piv[0])] + [jnp.where(at, 0.0, x) for x in piv[1:]]
                    piv = [y - mult * (x * now) for x, y in zip(lines, bases)]
                    for i in left:
                        cols[i] = jnp.where(at, 0.0, cols[i]) - mult * (row_of(cols[i], j) * now)
                rows[s] = piv
                if keep_ref is not None:
                    for spot, k in zip(spots, kept):
                        keep_ref[pl.ds(pl.multiple_of(base_row + s * SUB, SUB), SUB), pl.ds(spot, LANES)] = k
                spread = [[row_of(x, j) for j in range(SUB)] for x in piv]
                inside = (lane >= c0) & (lane < c0 + SUB)
                for g, mult in other.items():
                    new = list(rows[g])
                    new[0] = jnp.where(inside, 0.0, new[0])
                    for j in range(SUB):
                        new = [x - mult[j] * y[j] for x, y in zip(new, spread)]
                    rows[g] = new
            in_panel = (wide >= q * PANEL) & (wide < (q + 1) * PANEL)
            own = a_ref[:, pl.ds(own_at, LANES)]
            a_ref[:, pl.ds(own_at, LANES)] = jnp.where(in_panel, 0.0, own)
            l1, l2, l3 = thirds(jnp.where(in_panel, own, 0.0))
            l12 = jnp.concatenate([l1, l2], axis=1)
            l31 = jnp.concatenate([l3, l1], axis=1)
            for t, spot in enumerate(spots):
                r1, r2, r3 = thirds(jnp.concatenate([rows[g][t] for g in range(groups)], axis=0))
                above = jnp.zeros((q * PANEL, LANES), jnp.bfloat16)
                below = jnp.zeros((LANES - (q + 1) * PANEL, LANES), jnp.bfloat16)

                def tall(x, y):
                    parts = [above, x, below, above, y, below]
                    return jnp.concatenate([p for p in parts if p.shape[0]], axis=0)

                change = bdot(l12, tall(r1, r1)) + (bdot(l12, tall(r2, r2)) + bdot(l31, tall(r1, r3)))
                a_ref[:, pl.ds(spot, LANES)] = a_ref[:, pl.ds(spot, LANES)] - change
            for g in range(groups):
                for spot, x in zip(spots, rows[g]):
                    a_ref[pl.ds(pl.multiple_of(base_row + g * SUB, SUB), SUB), pl.ds(spot, LANES)] = x
        return carry

    lax.fori_loop(0, tiles, tile_step, 0)


def unit_rest(n, rank):
    return jnp.where((iota((n, n), 0) == iota((n, n), 1)) & (iota((n, n), 0) >= rank), 1.0, 0.0)


def both(n, rank_row, rank_col, x):
    return jnp.where((iota((n, n), 0) < rank_row) & (iota((n, n), 1) < rank_col), x, 0.0)


def place():
    return lax.axis_index("outer") * lax.axis_size("inner") + lax.axis_index("inner")


def leaf_kernel(rank_ref, m_ref, v_ref, g_ref, a_ref):
    n = g_ref.shape[0]
    rank = rank_ref[0, place()]
    keep = iota((n, n), 1) < rank
    v1 = jnp.where(keep, v_ref[:n, :], 0.0)
    v2 = jnp.where(keep, v_ref[n:, :], 0.0)
    a_ref[...] = m_ref[n:, n:]
    eliminate(a_ref)
    m12 = m_ref[:n, n:]
    w = dot(m12, a_ref[...])
    t = dot(a_ref[...], v2)
    a_ref[...] = m_ref[:n, :n] - dot(w, m12, NT)
    y = v1 - dot(w, v2)
    eliminate(a_ref)
    g_ref[...] = dot(v2, t, TN) + dot(y, dot(a_ref[...], y), TN) + unit_rest(n, rank)


def invert_kernel(depth, rank_ref, g_ref, l_ref, a_ref):
    n = g_ref.shape[0]
    rank = rank_ref[depth, jnp.right_shift(place(), depth)]
    a_ref[...] = g_ref[...]
    eliminate(a_ref)
    l_ref[...] = both(n, rank, rank, a_ref[...])


def last_kernel(depth, rank_ref, g_ref, l_ref, e_ref, a_ref):
    n = g_ref.shape[0]
    rank = rank_ref[depth, jnp.right_shift(place(), depth)]
    a_ref[...] = g_ref[...]
    eliminate(a_ref, e_ref, reverse=True)
    l_ref[...] = both(n, rank, rank, a_ref[...])


def merge_kernel(depth, rank_ref, l_ref, gy_ref, mine_ref, theirs_ref, g_ref, a_ref):
    n = g_ref.shape[0]
    node = jnp.right_shift(place(), depth)
    rx, ry = rank_ref[depth, node], rank_ref[depth, jnp.bitwise_xor(node, 1)]
    rp = rank_ref[depth + 1, jnp.right_shift(node, 1)]
    couple = both(n, rx, ry, mine_ref[1] + theirs_ref[1].T)
    px = both(n, rx, rp, mine_ref[0])
    py = both(n, ry, rp, theirs_ref[0])
    gy = gy_ref[...]
    w = dot(couple, gy)
    a_ref[...] = l_ref[...] + unit_rest(n, rx) - dot(w, couple, NT)
    y = px - dot(w, py)
    t = dot(py, dot(gy, py), TN)
    eliminate(a_ref)
    g_ref[...] = t + dot(y, dot(a_ref[...], y), TN) + unit_rest(n, rp)


def top_kernel(depth, rank_ref, l_ref, e_ref, lo_ref, eo_ref, c_ref, co_ref, f_ref, a_ref, keep_ref):
    n = l_ref.shape[0]
    pos = lax.axis_index("outer")
    first = jnp.bitwise_and(pos, 1) == 0
    node = jnp.bitwise_and(pos, -2)
    ra, rb = rank_ref[depth, node], rank_ref[depth, node + 1]
    row, col = iota((n, n), 0), iota((n, n), 1)
    pick = jnp.where(first, 1, 0) + jnp.zeros((n, n), jnp.int32) > 0
    ca = jnp.where(pick, c_ref[...], co_ref[...])
    cb = jnp.where(pick, co_ref[...], c_ref[...])
    lb = jnp.where(pick, lo_ref[...], l_ref[...])
    e = jnp.where(pick, e_ref[...], eo_ref[...])
    couple = both(n, ra, rb, ca + cb.T)
    f21 = dot(couple, jnp.where(row >= col, e, 0.0), ((0,), (1,)))
    a_ref[...] = lb + unit_rest(n, rb) - dot(f21, f21, NT)
    eliminate(a_ref, keep_ref)
    upper = jnp.where(row < col, e, 0.0) + jnp.where(row == col, 1.0 / jnp.where(row == col, e, 1.0), 0.0)
    f_ref[:n, :n] = upper.T
    f_ref[:n, n:] = jnp.zeros((n, n), jnp.float32)
    f_ref[n:, :n] = f21
    f_ref[n:, n:] = jnp.where(row <= col, keep_ref[...], 0.0).T


def call(kernel, name, outs, n, ranks, *arrays, keep=False):
    vmem = pl.BlockSpec(memory_space=pltpu.VMEM)
    square = pltpu.VMEM((n, n), jnp.float32)
    return pl.pallas_call(
        kernel,
        name=name,
        out_shape=[jax.ShapeDtypeStruct(shape, jnp.float32) for shape in outs],
        in_specs=[pl.BlockSpec(memory_space=pltpu.SMEM)] + [vmem] * len(arrays),
        out_specs=[vmem] * len(outs),
        scratch_shapes=[square] * (2 if keep else 1),
        cost_estimate=pl.CostEstimate(flops=4 * 10**9, bytes_accessed=4 * 10**6, transcendentals=0),
    )(ranks, *arrays)


def partner(x, axis, bit):
    return lax.ppermute(x, axis, [(i, i ^ 1 << bit) for i in range(lax.axis_size(axis))])


def body(leaf_blocks, leaf_bases, local_gens, chain_gens, node_ranks):
    n = leaf_bases.shape[2]
    in_levels = chain_gens.shape[0]
    square = (n, n)
    gens = [local_gens[0]] + [chain_gens[d] for d in range(in_levels)]
    others = [partner(gens[d], "inner", d) for d in range(in_levels)]
    couple = gens[in_levels][1]
    other_couple = partner(couple, "outer", 0)
    g = call(leaf_kernel, "leaf", [square], n, node_ranks, leaf_blocks[0], leaf_bases[0])[0]
    reduced = []
    for depth in range(in_levels):
        g_other = partner(g, "inner", depth)
        mine = call(functools.partial(invert_kernel, depth), "invert", [square], n, node_ranks, g)[0]
        reduced.append(mine)
        merge = functools.partial(merge_kernel, depth)
        g = call(merge, "merge", [square], n, node_ranks, mine, g_other, gens[depth], others[depth])[0]
    last = functools.partial(last_kernel, in_levels)
    mine, roots = call(last, "last", [square, square], n, node_ranks, g)
    reduced.append(mine)
    other_mine, other_roots = partner((mine, roots), "outer", 0)
    top = functools.partial(top_kernel, in_levels)
    arrays = (mine, roots, other_mine, other_roots, couple, other_couple)
    factor = call(top, "top", [(2 * n, 2 * n)], n, node_ranks, *arrays, keep=True)[0]
    return (reduced[0][None], jnp.stack(reduced[1:], axis=0), factor)


def solution(mesh):
    return jax.shard_map(
        body,
        mesh=mesh,
        in_specs=(
            P(("outer", "inner"), None, None),
            P(("outer", "inner"), None, None),
            P(("outer", "inner"), None, None, None),
            P(("outer", "inner"), None, None, None),
            P(),
        ),
        out_specs=(
            P(("outer", "inner"), None, None),
            P(("outer", "inner"), None, None),
            P(("outer", "inner"), None),
        ),
        check_vma=False,
    )
```

```python
import functools

import jax
import jax.numpy as jnp
from jax import lax
from jax.experimental import pallas as pl
from jax.experimental.pallas import tpu as pltpu
from jax.sharding import PartitionSpec as P

LANES = 128
SUB = 8
PANEL = 32
HIGH = lax.Precision.HIGHEST


def dot(a, b, dims=((1,), (0,))):
    return lax.dot_general(a, b, (dims, ((), ())), precision=HIGH, preferred_element_type=jnp.float32)


NT = ((1,), (1,))
TN = ((0,), (0,))


def thirds(x):
    a = x.astype(jnp.bfloat16)
    x = x - a.astype(jnp.float32)
    b = x.astype(jnp.bfloat16)
    return a, b, (x - b.astype(jnp.float32)).astype(jnp.bfloat16)


def bdot(a, b):
    return jnp.dot(a, b, preferred_element_type=jnp.float32)


def iota(shape, axis):
    return lax.broadcasted_iota(jnp.int32, shape, axis)


def total(terms):
    while len(terms) > 1:
        terms = [a + b for a, b in zip(terms[::2], terms[1::2])]
    return terms[0]


def row_of(x, j):
    return jnp.broadcast_to(x[j : j + 1, :], x.shape)


def col_of(x, c):
    return jnp.broadcast_to(x[:, c : c + 1], x.shape)


def eliminate(a_ref, keep_ref=None, reverse=False):
    n = a_ref.shape[0]
    tiles = n // LANES
    groups = PANEL // SUB
    sub = iota((SUB, LANES), 0)
    lane = iota((SUB, LANES), 1)
    wide = iota((n, LANES), 1)

    def order(count):
        return range(count - 1, -1, -1) if reverse else range(count)

    def tile_step(step, carry):
        h = tiles - 1 - step if reverse else step
        own_at = pl.multiple_of(h * LANES, LANES)
        spots = [own_at] + [pl.multiple_of(lax.rem(h + t, tiles) * LANES, LANES) for t in range(1, tiles)]
        ahead = None
        panels = list(order(LANES // PANEL))
        for q in panels:
            base_row = pl.multiple_of(h * LANES + q * PANEL, PANEL)
            rows = [
                [a_ref[pl.ds(pl.multiple_of(base_row + g * SUB, SUB), SUB), pl.ds(spot, LANES)] for spot in spots]
                for g in range(groups)
            ] if ahead is None else ahead
            for s in order(groups):
                c0 = q * PANEL + s * SUB
                cols = [col_of(rows[s][0], c0 + j) for j in range(SUB)]
                other = {g: [col_of(rows[g][0], c0 + j) for j in range(SUB)] for g in range(groups) if g != s}
                piv = list(rows[s])
                kept = [jnp.zeros((SUB, LANES), jnp.float32) for _ in spots]
                left = list(order(SUB))
                inv = 1.0 / row_of(cols[left[0]], left[0])
                while left:
                    j = left.pop(0)
                    here = lane == c0 + j
                    at = sub == j
                    lines = [row_of(x, j) for x in piv]
                    if keep_ref is not None:
                        root = lax.rsqrt(row_of(cols[j], j))
                        kept = [jnp.where(at, x * root, k) for x, k in zip(lines, kept)]
                    mult = jnp.where(at, -1.0, cols[j])
                    now = inv
                    if left:
                        i = left[0]
                        cross = row_of(cols[i], j)
                        inv = 1.0 / (row_of(cols[i], i) - (cross * now) * row_of(cols[j], i))
                    lines = [jnp.where(here, 1.0, lines[0])] + lines[1:]
                    bases = [jnp.where(at | here, 0.0, piv[0])] + [jnp.where(at, 0.0, x) for x in piv[1:]]
                    piv = [y - mult * (x * now) for x, y in zip(lines, bases)]
                    for i in left:
                        cols[i] = jnp.where(at, 0.0, cols[i]) - mult * (row_of(cols[i], j) * now)
                rows[s] = piv
                if keep_ref is not None:
                    for spot, k in zip(spots, kept):
                        keep_ref[pl.ds(pl.multiple_of(base_row + s * SUB, SUB), SUB), pl.ds(spot, LANES)] = k
                spread = [[row_of(x, j) for j in range(SUB)] for x in piv]
                inside = (lane >= c0) & (lane < c0 + SUB)
                for g, mult in other.items():
                    new = list(rows[g])
                    new[0] = jnp.where(inside, 0.0, new[0])
                    rows[g] = [x - total([mult[j] * y[j] for j in range(SUB)]) for x, y in zip(new, spread)]
            weights = []
            for t in range(tiles):
                r1, r2, r3 = thirds(jnp.concatenate([rows[g][t] for g in range(groups)], axis=0))
                above = jnp.zeros((q * PANEL, LANES), jnp.bfloat16)
                below = jnp.zeros((LANES - (q + 1) * PANEL, LANES), jnp.bfloat16)

                def tall(x, y):
                    parts = [above, x, below, above, y, below]
                    return jnp.concatenate([p for p in parts if p.shape[0]], axis=0)

                weights.append((tall(r1, r1), tall(r2, r2), tall(r1, r3)))

            def updated(at, count):
                inside = (wide[:count] >= q * PANEL) & (wide[:count] < (q + 1) * PANEL)
                own = a_ref[pl.ds(at, count), pl.ds(own_at, LANES)]
                l1, l2, l3 = thirds(jnp.where(inside, own, 0.0))
                l12 = jnp.concatenate([l1, l2], axis=1)
                l31 = jnp.concatenate([l3, l1], axis=1)
                olds = [jnp.where(inside, 0.0, own)] + [a_ref[pl.ds(at, count), pl.ds(spot, LANES)] for spot in spots[1:]]
                return [
                    old - (bdot(l12, w11) + (bdot(l12, w22) + bdot(l31, w13)))
                    for old, (w11, w22, w13) in zip(olds, weights)
                ]

            ahead = None
            if q != panels[-1]:
                onward = -PANEL if reverse else PANEL
                block = updated(pl.multiple_of(base_row + onward, PANEL), PANEL)
                ahead = [[x[g * SUB : (g + 1) * SUB] for x in block] for g in range(groups)]
            for spot, x in zip(spots, updated(0, n)):
                a_ref[:, pl.ds(spot, LANES)] = x
            for g in range(groups):
                for spot, x in zip(spots, rows[g]):
                    a_ref[pl.ds(pl.multiple_of(base_row + g * SUB, SUB), SUB), pl.ds(spot, LANES)] = x
        return carry

    lax.fori_loop(0, tiles, tile_step, 0)


def unit_rest(n, rank):
    return jnp.where((iota((n, n), 0) == iota((n, n), 1)) & (iota((n, n), 0) >= rank), 1.0, 0.0)


def both(n, rank_row, rank_col, x):
    return jnp.where((iota((n, n), 0) < rank_row) & (iota((n, n), 1) < rank_col), x, 0.0)


def place():
    return lax.axis_index("outer") * lax.axis_size("inner") + lax.axis_index("inner")


def leaf_kernel(rank_ref, m_ref, v_ref, g_ref, a_ref):
    n = g_ref.shape[0]
    rank = rank_ref[0, place()]
    keep = iota((n, n), 1) < rank
    v1 = jnp.where(keep, v_ref[:n, :], 0.0)
    v2 = jnp.where(keep, v_ref[n:, :], 0.0)
    a_ref[...] = m_ref[n:, n:]
    eliminate(a_ref)
    m12 = m_ref[:n, n:]
    w = dot(m12, a_ref[...])
    t = dot(a_ref[...], v2)
    a_ref[...] = m_ref[:n, :n] - dot(w, m12, NT)
    y = v1 - dot(w, v2)
    eliminate(a_ref)
    g_ref[...] = dot(v2, t, TN) + dot(y, dot(a_ref[...], y), TN) + unit_rest(n, rank)


def invert_kernel(depth, rank_ref, g_ref, l_ref, a_ref):
    n = g_ref.shape[0]
    rank = rank_ref[depth, jnp.right_shift(place(), depth)]
    a_ref[...] = g_ref[...]
    eliminate(a_ref)
    l_ref[...] = both(n, rank, rank, a_ref[...])


def last_kernel(depth, rank_ref, g_ref, l_ref, e_ref, a_ref):
    n = g_ref.shape[0]
    rank = rank_ref[depth, jnp.right_shift(place(), depth)]
    a_ref[...] = g_ref[...]
    eliminate(a_ref, e_ref, reverse=True)
    l_ref[...] = both(n, rank, rank, a_ref[...])


def merge_kernel(depth, rank_ref, l_ref, gy_ref, mine_ref, theirs_ref, g_ref, a_ref):
    n = g_ref.shape[0]
    node = jnp.right_shift(place(), depth)
    rx, ry = rank_ref[depth, node], rank_ref[depth, jnp.bitwise_xor(node, 1)]
    rp = rank_ref[depth + 1, jnp.right_shift(node, 1)]
    couple = both(n, rx, ry, mine_ref[1] + theirs_ref[1].T)
    px = both(n, rx, rp, mine_ref[0])
    py = both(n, ry, rp, theirs_ref[0])
    gy = gy_ref[...]
    w = dot(couple, gy)
    a_ref[...] = l_ref[...] + unit_rest(n, rx) - dot(w, couple, NT)
    y = px - dot(w, py)
    t = dot(py, dot(gy, py), TN)
    eliminate(a_ref)
    g_ref[...] = t + dot(y, dot(a_ref[...], y), TN) + unit_rest(n, rp)


def top_kernel(depth, rank_ref, l_ref, e_ref, lo_ref, eo_ref, c_ref, co_ref, f_ref, a_ref, keep_ref):
    n = l_ref.shape[0]
    pos = lax.axis_index("outer")
    first = jnp.bitwise_and(pos, 1) == 0
    node = jnp.bitwise_and(pos, -2)
    ra, rb = rank_ref[depth, node], rank_ref[depth, node + 1]
    row, col = iota((n, n), 0), iota((n, n), 1)
    pick = jnp.where(first, 1, 0) + jnp.zeros((n, n), jnp.int32) > 0
    ca = jnp.where(pick, c_ref[...], co_ref[...])
    cb = jnp.where(pick, co_ref[...], c_ref[...])
    lb = jnp.where(pick, lo_ref[...], l_ref[...])
    e = jnp.where(pick, e_ref[...], eo_ref[...])
    couple = both(n, ra, rb, ca + cb.T)
    f21 = dot(couple, jnp.where(row >= col, e, 0.0), ((0,), (1,)))
    a_ref[...] = lb + unit_rest(n, rb) - dot(f21, f21, NT)
    eliminate(a_ref, keep_ref)
    upper = jnp.where(row < col, e, 0.0) + jnp.where(row == col, 1.0 / jnp.where(row == col, e, 1.0), 0.0)
    f_ref[:n, :n] = upper.T
    f_ref[:n, n:] = jnp.zeros((n, n), jnp.float32)
    f_ref[n:, :n] = f21
    f_ref[n:, n:] = jnp.where(row <= col, keep_ref[...], 0.0).T


def call(kernel, name, outs, n, ranks, *arrays, keep=False):
    vmem = pl.BlockSpec(memory_space=pltpu.VMEM)
    square = pltpu.VMEM((n, n), jnp.float32)
    return pl.pallas_call(
        kernel,
        name=name,
        out_shape=[jax.ShapeDtypeStruct(shape, jnp.float32) for shape in outs],
        in_specs=[pl.BlockSpec(memory_space=pltpu.SMEM)] + [vmem] * len(arrays),
        out_specs=[vmem] * len(outs),
        scratch_shapes=[square] * (2 if keep else 1),
        cost_estimate=pl.CostEstimate(flops=4 * 10**9, bytes_accessed=4 * 10**6, transcendentals=0),
    )(ranks, *arrays)


def partner(x, axis, bit):
    return lax.ppermute(x, axis, [(i, i ^ 1 << bit) for i in range(lax.axis_size(axis))])


def body(leaf_blocks, leaf_bases, local_gens, chain_gens, node_ranks):
    n = leaf_bases.shape[2]
    in_levels = chain_gens.shape[0]
    square = (n, n)
    gens = [local_gens[0]] + [chain_gens[d] for d in range(in_levels)]
    others = [partner(gens[d], "inner", d) for d in range(in_levels)]
    couple = gens[in_levels][1]
    other_couple = partner(couple, "outer", 0)
    g = call(leaf_kernel, "leaf", [square], n, node_ranks, leaf_blocks[0], leaf_bases[0])[0]
    reduced = []
    for depth in range(in_levels):
        g_other = partner(g, "inner", depth)
        mine = call(functools.partial(invert_kernel, depth), "invert", [square], n, node_ranks, g)[0]
        reduced.append(mine)
        merge = functools.partial(merge_kernel, depth)
        g = call(merge, "merge", [square], n, node_ranks, mine, g_other, gens[depth], others[depth])[0]
    last = functools.partial(last_kernel, in_levels)
    mine, roots = call(last, "last", [square, square], n, node_ranks, g)
    reduced.append(mine)
    other_mine, other_roots = partner((mine, roots), "outer", 0)
    top = functools.partial(top_kernel, in_levels)
    arrays = (mine, roots, other_mine, other_roots, couple, other_couple)
    factor = call(top, "top", [(2 * n, 2 * n)], n, node_ranks, *arrays, keep=True)[0]
    return (reduced[0][None], jnp.stack(reduced[1:], axis=0), factor)


def solution(mesh):
    return jax.shard_map(
        body,
        mesh=mesh,
        in_specs=(
            P(("outer", "inner"), None, None),
            P(("outer", "inner"), None, None),
            P(("outer", "inner"), None, None, None),
            P(("outer", "inner"), None, None, None),
            P(),
        ),
        out_specs=(
            P(("outer", "inner"), None, None),
            P(("outer", "inner"), None, None),
            P(("outer", "inner"), None),
        ),
        check_vma=False,
    )
```

```python
import functools

import jax
import jax.numpy as jnp
from jax import lax
from jax.experimental import pallas as pl
from jax.experimental.pallas import tpu as pltpu
from jax.sharding import PartitionSpec as P

LANES = 128
SUB = 8
PANEL = 32
HIGH = lax.Precision.HIGHEST


def dot(a, b, dims=((1,), (0,))):
    return lax.dot_general(a, b, (dims, ((), ())), precision=HIGH, preferred_element_type=jnp.float32)


NT = ((1,), (1,))
TN = ((0,), (0,))


def thirds(x):
    a = x.astype(jnp.bfloat16)
    x = x - a.astype(jnp.float32)
    b = x.astype(jnp.bfloat16)
    return a, b, (x - b.astype(jnp.float32)).astype(jnp.bfloat16)


def bdot(a, b):
    return jnp.dot(a, b, preferred_element_type=jnp.float32)


def iota(shape, axis):
    return lax.broadcasted_iota(jnp.int32, shape, axis)


def total(terms):
    while len(terms) > 1:
        terms = [a + b for a, b in zip(terms[::2], terms[1::2])]
    return terms[0]


def row_of(x, j):
    return jnp.broadcast_to(x[j : j + 1, :], x.shape)


def col_of(x, c):
    return jnp.broadcast_to(x[:, c : c + 1], x.shape)


def eliminate(a_ref, keep_ref=None, reverse=False):
    n = a_ref.shape[0]
    tiles = n // LANES
    groups = PANEL // SUB
    sub = iota((SUB, LANES), 0)
    lane = iota((SUB, LANES), 1)
    wide = iota((n, LANES), 1)

    def order(count):
        return range(count - 1, -1, -1) if reverse else range(count)

    def tile_step(step, carry):
        h = tiles - 1 - step if reverse else step
        own_at = pl.multiple_of(h * LANES, LANES)
        spots = [own_at] + [pl.multiple_of(lax.rem(h + t, tiles) * LANES, LANES) for t in range(1, tiles)]
        ahead = None
        panels = list(order(LANES // PANEL))
        for q in panels:
            base_row = pl.multiple_of(h * LANES + q * PANEL, PANEL)
            rows = [
                [a_ref[pl.ds(pl.multiple_of(base_row + g * SUB, SUB), SUB), pl.ds(spot, LANES)] for spot in spots]
                for g in range(groups)
            ] if ahead is None else ahead
            for s in order(groups):
                c0 = q * PANEL + s * SUB
                cols = [col_of(rows[s][0], c0 + j) for j in range(SUB)]
                other = {g: [col_of(rows[g][0], c0 + j) for j in range(SUB)] for g in range(groups) if g != s}
                piv = list(rows[s])
                kept = [jnp.zeros((SUB, LANES), jnp.float32) for _ in spots]
                left = list(order(SUB))
                inv = 1.0 / row_of(cols[left[0]], left[0])
                while left:
                    j = left.pop(0)
                    here = lane == c0 + j
                    at = sub == j
                    lines = [row_of(x, j) for x in piv]
                    if keep_ref is not None:
                        root = lax.rsqrt(row_of(cols[j], j))
                        kept = [jnp.where(at, x * root, k) for x, k in zip(lines, kept)]
                    mult = jnp.where(at, -1.0, cols[j])
                    now = inv
                    if left:
                        i = left[0]
                        cross = row_of(cols[i], j)
                        inv = 1.0 / (row_of(cols[i], i) - (cross * now) * row_of(cols[j], i))
                    lines = [jnp.where(here, 1.0, lines[0])] + lines[1:]
                    bases = [jnp.where(at | here, 0.0, piv[0])] + [jnp.where(at, 0.0, x) for x in piv[1:]]
                    piv = [y - mult * (x * now) for x, y in zip(lines, bases)]
                    for i in left:
                        cols[i] = jnp.where(at, 0.0, cols[i]) - mult * (row_of(cols[i], j) * now)
                rows[s] = piv
                if keep_ref is not None:
                    for spot, k in zip(spots, kept):
                        keep_ref[pl.ds(pl.multiple_of(base_row + s * SUB, SUB), SUB), pl.ds(spot, LANES)] = k
                spread = [[row_of(x, j) for j in range(SUB)] for x in piv]
                inside = (lane >= c0) & (lane < c0 + SUB)
                for g, mult in other.items():
                    new = list(rows[g])
                    new[0] = jnp.where(inside, 0.0, new[0])
                    rows[g] = [x - total([mult[j] * y[j] for j in range(SUB)]) for x, y in zip(new, spread)]
            weights = []
            for t in range(tiles):
                r1, r2, r3 = thirds(jnp.concatenate([rows[g][t] for g in range(groups)], axis=0))
                blank = jnp.zeros((LANES - 2 * PANEL, LANES), jnp.bfloat16)
                weights.append(jnp.concatenate([r1, r1, r2, r2, r1, r3, blank], axis=0))

            def updated(at, count):
                inside = (wide[:count] >= q * PANEL) & (wide[:count] < (q + 1) * PANEL)
                own = a_ref[pl.ds(at, count), pl.ds(own_at, LANES)]
                olds = [jnp.where(inside, 0.0, own)] + [a_ref[pl.ds(at, count), pl.ds(spot, LANES)] for spot in spots[1:]]
                x = jnp.where(inside, own, 0.0)
                x = x + pltpu.roll(x, PANEL, 1)
                x = x + pltpu.roll(x, 2 * PANEL, 1)
                l1 = x.astype(jnp.bfloat16).astype(jnp.float32)
                l2 = (x - l1).astype(jnp.bfloat16).astype(jnp.float32)
                l3 = x - l1 - l2
                at_quarter = wide[:count] // PANEL
                one = jnp.where((at_quarter & 1) == 0, l1, l2)
                two = jnp.where(at_quarter == 0, l3, jnp.where(at_quarter == 1, l1, 0.0))
                lhs = jnp.concatenate([one.astype(jnp.bfloat16), two.astype(jnp.bfloat16)], axis=1)
                return [old - bdot(lhs, w) for old, w in zip(olds, weights)]

            ahead = None
            if q != panels[-1]:
                onward = -PANEL if reverse else PANEL
                block = updated(pl.multiple_of(base_row + onward, PANEL), PANEL)
                ahead = [[x[g * SUB : (g + 1) * SUB] for x in block] for g in range(groups)]
            for spot, x in zip(spots, updated(0, n)):
                a_ref[:, pl.ds(spot, LANES)] = x
            for g in range(groups):
                for spot, x in zip(spots, rows[g]):
                    a_ref[pl.ds(pl.multiple_of(base_row + g * SUB, SUB), SUB), pl.ds(spot, LANES)] = x
        return carry

    lax.fori_loop(0, tiles, tile_step, 0)


def unit_rest(n, rank):
    return jnp.where((iota((n, n), 0) == iota((n, n), 1)) & (iota((n, n), 0) >= rank), 1.0, 0.0)


def both(n, rank_row, rank_col, x):
    return jnp.where((iota((n, n), 0) < rank_row) & (iota((n, n), 1) < rank_col), x, 0.0)


def place():
    return lax.axis_index("outer") * lax.axis_size("inner") + lax.axis_index("inner")


def leaf_kernel(rank_ref, m_ref, v_ref, g_ref, a_ref):
    n = g_ref.shape[0]
    rank = rank_ref[0, place()]
    keep = iota((n, n), 1) < rank
    v1 = jnp.where(keep, v_ref[:n, :], 0.0)
    v2 = jnp.where(keep, v_ref[n:, :], 0.0)
    a_ref[...] = m_ref[n:, n:]
    eliminate(a_ref)
    m12 = m_ref[:n, n:]
    w = dot(m12, a_ref[...])
    t = dot(a_ref[...], v2)
    a_ref[...] = m_ref[:n, :n] - dot(w, m12, NT)
    y = v1 - dot(w, v2)
    eliminate(a_ref)
    g_ref[...] = dot(v2, t, TN) + dot(y, dot(a_ref[...], y), TN) + unit_rest(n, rank)


def invert_kernel(depth, rank_ref, g_ref, l_ref, a_ref):
    n = g_ref.shape[0]
    rank = rank_ref[depth, jnp.right_shift(place(), depth)]
    a_ref[...] = g_ref[...]
    eliminate(a_ref)
    l_ref[...] = both(n, rank, rank, a_ref[...])


def last_kernel(depth, rank_ref, g_ref, l_ref, e_ref, a_ref):
    n = g_ref.shape[0]
    rank = rank_ref[depth, jnp.right_shift(place(), depth)]
    a_ref[...] = g_ref[...]
    eliminate(a_ref, e_ref, reverse=True)
    l_ref[...] = both(n, rank, rank, a_ref[...])


def merge_kernel(depth, rank_ref, l_ref, gy_ref, mine_ref, theirs_ref, g_ref, a_ref):
    n = g_ref.shape[0]
    node = jnp.right_shift(place(), depth)
    rx, ry = rank_ref[depth, node], rank_ref[depth, jnp.bitwise_xor(node, 1)]
    rp = rank_ref[depth + 1, jnp.right_shift(node, 1)]
    couple = both(n, rx, ry, mine_ref[1] + theirs_ref[1].T)
    px = both(n, rx, rp, mine_ref[0])
    py = both(n, ry, rp, theirs_ref[0])
    gy = gy_ref[...]
    w = dot(couple, gy)
    a_ref[...] = l_ref[...] + unit_rest(n, rx) - dot(w, couple, NT)
    y = px - dot(w, py)
    t = dot(py, dot(gy, py), TN)
    eliminate(a_ref)
    g_ref[...] = t + dot(y, dot(a_ref[...], y), TN) + unit_rest(n, rp)


def top_kernel(depth, rank_ref, l_ref, e_ref, lo_ref, eo_ref, c_ref, co_ref, f_ref, a_ref, keep_ref):
    n = l_ref.shape[0]
    pos = lax.axis_index("outer")
    first = jnp.bitwise_and(pos, 1) == 0
    node = jnp.bitwise_and(pos, -2)
    ra, rb = rank_ref[depth, node], rank_ref[depth, node + 1]
    row, col = iota((n, n), 0), iota((n, n), 1)
    pick = jnp.where(first, 1, 0) + jnp.zeros((n, n), jnp.int32) > 0
    ca = jnp.where(pick, c_ref[...], co_ref[...])
    cb = jnp.where(pick, co_ref[...], c_ref[...])
    lb = jnp.where(pick, lo_ref[...], l_ref[...])
    e = jnp.where(pick, e_ref[...], eo_ref[...])
    couple = both(n, ra, rb, ca + cb.T)
    f21 = dot(couple, jnp.where(row >= col, e, 0.0), ((0,), (1,)))
    a_ref[...] = lb + unit_rest(n, rb) - dot(f21, f21, NT)
    eliminate(a_ref, keep_ref)
    upper = jnp.where(row < col, e, 0.0) + jnp.where(row == col, 1.0 / jnp.where(row == col, e, 1.0), 0.0)
    f_ref[:n, :n] = upper.T
    f_ref[:n, n:] = jnp.zeros((n, n), jnp.float32)
    f_ref[n:, :n] = f21
    f_ref[n:, n:] = jnp.where(row <= col, keep_ref[...], 0.0).T


def call(kernel, name, outs, n, ranks, *arrays, keep=False):
    vmem = pl.BlockSpec(memory_space=pltpu.VMEM)
    square = pltpu.VMEM((n, n), jnp.float32)
    return pl.pallas_call(
        kernel,
        name=name,
        out_shape=[jax.ShapeDtypeStruct(shape, jnp.float32) for shape in outs],
        in_specs=[pl.BlockSpec(memory_space=pltpu.SMEM)] + [vmem] * len(arrays),
        out_specs=[vmem] * len(outs),
        scratch_shapes=[square] * (2 if keep else 1),
        cost_estimate=pl.CostEstimate(flops=4 * 10**9, bytes_accessed=4 * 10**6, transcendentals=0),
    )(ranks, *arrays)


def partner(x, axis, bit):
    return lax.ppermute(x, axis, [(i, i ^ 1 << bit) for i in range(lax.axis_size(axis))])


def body(leaf_blocks, leaf_bases, local_gens, chain_gens, node_ranks):
    n = leaf_bases.shape[2]
    in_levels = chain_gens.shape[0]
    square = (n, n)
    gens = [local_gens[0]] + [chain_gens[d] for d in range(in_levels)]
    others = [partner(gens[d], "inner", d) for d in range(in_levels)]
    couple = gens[in_levels][1]
    other_couple = partner(couple, "outer", 0)
    g = call(leaf_kernel, "leaf", [square], n, node_ranks, leaf_blocks[0], leaf_bases[0])[0]
    reduced = []
    for depth in range(in_levels):
        g_other = partner(g, "inner", depth)
        mine = call(functools.partial(invert_kernel, depth), "invert", [square], n, node_ranks, g)[0]
        reduced.append(mine)
        merge = functools.partial(merge_kernel, depth)
        g = call(merge, "merge", [square], n, node_ranks, mine, g_other, gens[depth], others[depth])[0]
    last = functools.partial(last_kernel, in_levels)
    mine, roots = call(last, "last", [square, square], n, node_ranks, g)
    reduced.append(mine)
    other_mine, other_roots = partner((mine, roots), "outer", 0)
    top = functools.partial(top_kernel, in_levels)
    arrays = (mine, roots, other_mine, other_roots, couple, other_couple)
    factor = call(top, "top", [(2 * n, 2 * n)], n, node_ranks, *arrays, keep=True)[0]
    return (reduced[0][None], jnp.stack(reduced[1:], axis=0), factor)


def solution(mesh):
    return jax.shard_map(
        body,
        mesh=mesh,
        in_specs=(
            P(("outer", "inner"), None, None),
            P(("outer", "inner"), None, None),
            P(("outer", "inner"), None, None, None),
            P(("outer", "inner"), None, None, None),
            P(),
        ),
        out_specs=(
            P(("outer", "inner"), None, None),
            P(("outer", "inner"), None, None),
            P(("outer", "inner"), None),
        ),
        check_vma=False,
    )
```
